128 devices in a mesh: dp: 2 (over y_hi), corpus: 16 (over y_lo, x, core), tensor: 4 (over z).
Axes of the slice: x: 4, y: 4 (y_hi: 2, y_lo: 2; y = y_hi * 2 + y_lo), z: 4, core: 2. Of those that a mesh axis runs over, the one named last changes fastest.
Arguments:
- hidden: bfloat16 [16384, 4096], P(('dp', 'corpus')), may hold values from -6 to 6
- norm_gain: bfloat16 [4096], replicated, may hold values from 0.099609375 to 1.8984375
- query_weight: bfloat16 [4096, 4096], P('corpus', 'tensor'), may hold values from -0.1875 to 0.1875
- output_weight: bfloat16 [4096, 4096], P('tensor'), may hold values from -0.375 to 0.375
- cache: bfloat16 [2, 32768, 1024], P(None, 'corpus', 'tensor'), may hold values from -240 to 240
- pattern: int32 [128, 16], P(('dp', 'corpus')), may hold values from 0 to 255, as said below
Outputs:
- scored: bfloat16 [16384, 4096], P(('dp', 'corpus', 'tensor'))
The draws below stay inside these ranges and needn't reach their ends.
Inputs may be any that keep to these rules, and one draw needn't show every extreme that they name: Passage block j lies on index j // 16 of corpus. The 4 rows of pattern of one index of dp and corpus name blocks of exactly half of the indices of corpus, each of those exactly 8 times, repeats counted.
All inputs are finite; a program needn't handle non-finite values.
Results may differ from the reference program's by a relative error of at most 0.0075.
The reference program's roundings to bfloat16 on the way (of `normed`, `queries`, `probs` and `attended`) count: a program that leaves them out, or rounds other values in their place, can miss the bound.
Values may be sent and summed in bfloat16 or wider, within the bound.
No kernel may reach another device: no remote copies, remote signals or barrier semaphores. Data moves between devices by JAX's collectives and lax.ppermute only.
A program may use at most 128 MiB of HBM per device.

```python
import math
import jax
import jax.numpy as jnp
from jax import lax

D = 4096
H = 32
KVH = 8
HD = 128
BLOCK = 128
CAND = 16
QB_DEV = 4
BLK_DEV = 16
QBLK = 128
QROWS = 16384
NBLK = 256
PASS = 32768
MOST = 8
N_DP = 2
N_CORPUS = 16


def draw_cache(key, part):
    first = jax.random.fold_in(key, 0)
    base = jax.random.truncated_normal(first, -4.0, 4.0, (2, PASS, KVH * HD), jnp.float32)
    return base.astype(jnp.bfloat16)


def draw_pattern(key, part):
    groups = N_DP * N_CORPUS
    slot_total = QB_DEV * CAND
    first, second, third = jax.random.split(key, 3)
    orders = jax.vmap(lambda sub: jax.random.permutation(sub, N_CORPUS))(jax.random.split(first, groups))
    sorted_owner = jnp.take(orders, jnp.arange(slot_total) // MOST, axis=1)
    shuffles = jax.vmap(lambda sub: jax.random.permutation(sub, slot_total))(jax.random.split(second, groups))
    owners = jnp.take_along_axis(sorted_owner, shuffles, axis=1)
    within = jax.random.randint(third, (groups, slot_total), 0, BLK_DEV)
    blocks = owners * BLK_DEV + within
    return blocks.reshape(groups * QB_DEV, CAND).astype(jnp.int32)


def level_of(rng, shape, cuts, least, high):
    def one(axis_at, shards_of):
        steps = jax.random.uniform(jax.random.fold_in(jax.random.fold_in(rng, 6), axis_at), (shards_of,), jnp.float32, least / len(cuts), high / len(cuts))
        return jnp.repeat(jnp.exp(steps), shape[axis_at] // shards_of).reshape((-1,) + (1,) * (len(shape) - axis_at - 1))

    loudness = one(*cuts[0])
    for cut in cuts[1:]:
        loudness = loudness * one(*cut)
    return loudness


def centred(own_key, extent, spread, most, cuts=(), held_as=jnp.bfloat16):
    array = spread * jax.random.normal(own_key, extent, jnp.float32)
    if cuts:
        array = array * level_of(own_key, extent, cuts, -0.22, 0.18)
    return jnp.clip(array, -most, most).astype(held_as)


def setup_inputs(seed: int = 0) -> dict:
    arg_keys = jax.random.split(jax.random.key(seed), 7)
    return {
        "hidden": centred(arg_keys[0], (QROWS, D), 1.0, 6.0, ((0, 32),)),
        "norm_gain": jnp.clip(1.0 + 0.18 * jax.random.normal(arg_keys[1], (D,), jnp.float32), 0.099609375, 1.8984375).astype(jnp.bfloat16),
        "query_weight": centred(arg_keys[2], (D, H * HD), (D // 4) ** -0.5, 0.1875, ((0, 16), (1, 4))),
        "output_weight": centred(arg_keys[3], (H * HD, D), (H * HD // 16) ** -0.5, 0.375, ((0, 4),)),
        "cache": draw_cache(jax.random.fold_in(arg_keys[6], 71), 0),
        "pattern": draw_pattern(jax.random.fold_in(arg_keys[6], 71), 0),
    }


def reference(hidden, norm_gain, query_weight, output_weight, cache, pattern):
    widened = hidden.astype(jnp.float32)
    meansq = lax.optimization_barrier(jnp.mean(widened * widened, axis=-1, keepdims=True))
    normed = (widened * lax.rsqrt(meansq + 1e-05) * norm_gain.astype(jnp.float32)).astype(jnp.bfloat16)
    factor = 1.0 / math.sqrt(HD)
    queries = (jnp.dot(normed, query_weight, preferred_element_type=jnp.float32) * factor).astype(jnp.bfloat16)
    query_tiles = queries.reshape(QBLK, BLOCK, KVH, H // KVH, HD)
    key_tiles = cache[0].reshape(NBLK, BLOCK, KVH, HD)
    value_tiles = cache[1].reshape(NBLK, BLOCK, KVH, HD)

    def attend(operands):
        query_tile, chosen = operands
        chosen = chosen.astype(jnp.int32)
        keys_here = jnp.take(key_tiles, chosen, axis=0).reshape(CAND * BLOCK, KVH, HD).astype(jnp.float32)
        values_here = jnp.take(value_tiles, chosen, axis=0).reshape(CAND * BLOCK, KVH, HD).astype(jnp.float32)
        scores = jnp.einsum('rkgd,skd->kgrs', query_tile.astype(jnp.float32), keys_here)
        highest = lax.optimization_barrier(jnp.max(scores, axis=-1, keepdims=True))
        weights = jnp.exp(scores - highest)
        totals = lax.optimization_barrier(jnp.sum(weights, axis=-1, keepdims=True))
        probs = weights.astype(jnp.bfloat16).astype(jnp.float32)
        mixed = jnp.einsum('kgrs,skd->kgrd', probs, values_here) / totals
        return jnp.transpose(mixed, (2, 0, 1, 3)).reshape(BLOCK, H * HD).astype(jnp.bfloat16)
    attended = lax.map(attend, (query_tiles, pattern)).reshape(QROWS, H * HD)
    return jnp.dot(attended, output_weight, preferred_element_type=jnp.float32).astype(jnp.bfloat16)
```

```python
import functools
import math

import jax
import jax.numpy as jnp
from jax import lax
from jax.experimental import pallas as pl
from jax.experimental.pallas import tpu as pltpu
from jax.sharding import PartitionSpec as P

HD = 128
BLOCK = 128
NX = 4
NY = 4
NZ = 4
AXES = ("dp", "corpus", "tensor")
LOW = -3.0e38
VMEM_LIMIT = 60 * 1024 * 1024


def device_index(x, y, z, core):
    return (((y // 2) * 2 + y % 2) * NX + x) * 2 * NZ + core * NZ + z


def shift(value, dx=0, dy=0, dz=0, dk=0):
    pairs = []
    for x in range(NX):
        for y in range(NY):
            for z in range(NZ):
                for core in range(2):
                    target = device_index((x + dx) % NX, (y + dy) % NY, (z + dz) % NZ, (core + dk) % 2)
                    pairs.append((device_index(x, y, z, core), target))
    return lax.ppermute(value, AXES, pairs)


def any_spec():
    return pl.BlockSpec(memory_space=pl.ANY)


def vmem_spec():
    return pl.BlockSpec(memory_space=pltpu.VMEM)


def smem_spec():
    return pl.BlockSpec(memory_space=pltpu.SMEM)


def project_kernel(count, where_ref, normed_ref, *refs):
    pieces = refs[:count]
    first_ref, second_ref = refs[count : count + 2]
    weight, sems = refs[count + 2 :]
    copies = []
    for at, piece in enumerate(pieces):
        rows = piece.shape[0]
        start = pl.multiple_of(where_ref[at], BLOCK)
        copy = pltpu.make_async_copy(piece, weight.at[pl.ds(start, rows), :], sems.at[at])
        copy.start()
        copies.append(copy)
    for copy in copies:
        copy.wait()
    factor = 1.0 / math.sqrt(HD)
    width = 256
    for at in range(weight.shape[1] // width):
        got = jnp.dot(
            normed_ref[...],
            weight[:, at * width : (at + 1) * width],
            preferred_element_type=jnp.float32,
        )
        got = (got * factor).astype(jnp.bfloat16)
        for half in range(width // HD):
            head = at * (width // HD) + half
            target = first_ref if head < 4 else second_ref
            for block in range(4):
                target[block, (head % 4) * BLOCK : (head % 4 + 1) * BLOCK, :] = got[
                    block * BLOCK : (block + 1) * BLOCK, half * HD : (half + 1) * HD
                ]


def project(where, normed, pieces):
    count = len(pieces)
    out = jax.ShapeDtypeStruct((4, 4 * BLOCK, HD), jnp.bfloat16)
    depth = normed.shape[1]
    columns = pieces[0].shape[1]
    return pl.pallas_call(
        functools.partial(project_kernel, count),
        out_shape=(out, out),
        in_specs=[smem_spec(), vmem_spec()] + [any_spec()] * count,
        out_specs=(vmem_spec(), vmem_spec()),
        scratch_shapes=[
            pltpu.VMEM((depth, columns), jnp.bfloat16),
            pltpu.SemaphoreType.DMA((count,)),
        ],
        compiler_params=pltpu.CompilerParams(vmem_limit_bytes=VMEM_LIMIT),
        cost_estimate=pl.CostEstimate(
            flops=2 * 512 * depth * columns, bytes_accessed=14 << 20, transcendentals=0
        ),
        name="project",
    )(where, normed, *pieces)


def attend_kernel(distances, offsets, first, last, here_ref, pattern_ref, *refs):
    arrays = 2 * len(distances)
    blocks = len(offsets)
    units = 4 * blocks
    refs = list(refs)
    q_refs = [refs.pop(0) for _ in range(4)]
    kv_refs = [refs.pop(0) for _ in range(arrays)]
    if not first:
        acc_in, stat_in = refs.pop(0), refs.pop(0)
    if last:
        own_ref, own_stat, part0_ref, part1_ref, part_stat = [refs.pop(0) for _ in range(5)]
    else:
        acc_out, stat_out = refs.pop(0), refs.pop(0)
    q_all, keys, values, acc, stats, high, total, lists, counts, q_sem, k_sem, s_sem = refs
    my_x, my_y, tensor = here_ref[0], here_ref[1], here_ref[2]

    copies = []
    for kind in range(4):
        for at, offset in enumerate(offsets):
            block = lax.rem(tensor + offset, 4)
            copy = pltpu.make_async_copy(
                q_refs[kind].at[block], q_all.at[kind * blocks + at], q_sem.at[kind * blocks + at]
            )
            copy.start()
            copies.append(copy)
    if not first:
        for kind in range(4):
            for at, offset in enumerate(offsets):
                slot = kind * 4 + (2, 1, 3, 0).index(offset)
                for source, target, which in ((acc_in, acc, 0), (stat_in, stats, 1)):
                    copy = pltpu.make_async_copy(
                        source.at[slot],
                        target.at[kind * blocks + at],
                        s_sem.at[which, kind * blocks + at],
                    )
                    copy.start()
                    copies.append(copy)
    for at in range(arrays):
        for head in range(2):
            for which, target in ((0, keys), (1, values)):
                copy = pltpu.make_async_copy(
                    kv_refs[at].at[which, :, head * HD : (head + 1) * HD],
                    target.at[head, at * 2048 : (at + 1) * 2048, :],
                    k_sem.at[at, head, which],
                )
                copy.start()
                copies.append(copy)

    my_core = here_ref[3]

    def scan_row(row, _):
        def scan_one(at, found):
            named = pattern_ref[row, at]
            owner = named // 16
            matches = (owner // 8) == my_y
            away = lax.rem((owner // 2) % 4 - my_x + 4, 4)
            place = jnp.int32(0)
            inside = jnp.bool_(False)
            for number, distance in enumerate(distances):
                hit = away == distance
                inside = inside | hit
                place = jnp.where(hit, number, place)
            other = jnp.where(owner % 2 == my_core, 0, 1)
            lists[row, found] = (place * 2 + other) * 16 + named % 16
            return found + jnp.where(matches & inside, 1, 0)

        counts[row] = lax.fori_loop(0, 16, scan_one, jnp.int32(0))
        return 0

    lax.fori_loop(0, 12, scan_row, 0)
    for copy in copies:
        copy.wait()

    rows = 4 * BLOCK

    def one_unit(unit, _):
        kind = unit // blocks
        at = unit % blocks
        offset = jnp.int32(offsets[0])
        for number in range(1, blocks):
            offset = jnp.where(at == number, offsets[number], offset)
        block = lax.rem(tensor + offset, 4)
        row = jnp.where(kind < 2, 0, (kind - 1) * 4) + block
        head = kind % 2
        if first:
            acc[unit] = jnp.zeros((rows, HD), jnp.float32)
            high[...] = jnp.full((rows, HD), LOW, jnp.float32)
            total[...] = jnp.zeros((rows, HD), jnp.float32)
        else:
            lane = lax.broadcasted_iota(jnp.int32, (BLOCK, HD), 1)
            for part in range(4):
                span = slice(part * BLOCK, (part + 1) * BLOCK)
                high[span, :] = jnp.transpose(
                    jnp.broadcast_to(stats[unit, 0:1, span], (BLOCK, BLOCK))
                )
                sums = jnp.transpose(jnp.broadcast_to(stats[unit, 1:2, span], (BLOCK, BLOCK)))
                total[span, :] = jnp.where(lane == 0, sums, 0.0)
        found = counts[row]

        def one_pair(pair, _):
            left = lists[row, 2 * pair]
            valid = 2 * pair + 1 < found
            right = lists[row, jnp.where(valid, 2 * pair + 1, 2 * pair)]
            left = pl.multiple_of(left * BLOCK, BLOCK)
            right = pl.multiple_of(right * BLOCK, BLOCK)
            k2 = jnp.concatenate(
                [keys[head, pl.ds(left, BLOCK), :], keys[head, pl.ds(right, BLOCK), :]], axis=0
            )
            v2 = jnp.concatenate(
                [values[head, pl.ds(left, BLOCK), :], values[head, pl.ds(right, BLOCK), :]], axis=0
            )
            for part in range(4):
                span = slice(part * BLOCK, (part + 1) * BLOCK)
                scores = lax.dot_general(
                    q_all[unit, span, :],
                    k2,
                    (((1,), (1,)), ((), ())),
                    preferred_element_type=jnp.float32,
                )
                s0 = scores[:, :BLOCK]
                s1 = jnp.where(valid, scores[:, BLOCK:], LOW)
                before = high[span, :]
                now = jnp.maximum(before, jnp.max(jnp.maximum(s0, s1), axis=1, keepdims=True))
                p0 = jnp.exp(s0 - now)
                p1 = jnp.exp(s1 - now)
                fade = jnp.exp(before - now)
                high[span, :] = now
                total[span, :] = total[span, :] * fade + (p0 + p1)
                probs = jnp.concatenate(
                    [p0.astype(jnp.bfloat16), p1.astype(jnp.bfloat16)], axis=1
                )
                acc[unit, span, :] = acc[unit, span, :] * fade + jnp.dot(
                    probs, v2, preferred_element_type=jnp.float32
                )
            return 0

        lax.fori_loop(0, (found + 1) // 2, one_pair, 0)

        lane = lax.broadcasted_iota(jnp.int32, (BLOCK, HD), 1)
        for part in range(4):
            span = slice(part * BLOCK, (part + 1) * BLOCK)
            sums = jnp.sum(total[span, :], axis=1, keepdims=True)
            both = jnp.transpose(jnp.where(lane < 64, high[span, :], sums))
            stats[unit, 0:1, span] = both[0:1, :]
            stats[unit, 1:2, span] = both[64:65, :]
            if last:
                total[span, :] = jnp.broadcast_to(sums, (BLOCK, HD))
        if last:

            @pl.when(kind < 2)
            def _():
                own_ref[kind * blocks + at] = acc[unit]
                own_stat[kind * blocks + at] = stats[unit]

            @pl.when(kind >= 2)
            def _():
                sums = total[...]
                share = jnp.where(
                    sums > 0.0, acc[unit] / jnp.where(sums > 0.0, sums, 1.0), 0.0
                ).astype(jnp.bfloat16)
                part_stat[kind - 2, at] = stats[unit]

                @pl.when(kind == 2)
                def _():
                    part0_ref[at] = share

                @pl.when(kind == 3)
                def _():
                    part1_ref[at] = share

        else:
            acc_out[unit] = acc[unit]
            stat_out[unit] = stats[unit]
        return 0

    lax.fori_loop(0, units, one_unit, 0)


def attend(here, patterns, queries, arrays, distances, offsets, state=None, last=False):
    blocks = len(offsets)
    units = 4 * blocks
    rows = 4 * BLOCK
    f32 = jnp.float32
    if last:
        out_shape = (
            jax.ShapeDtypeStruct((2 * blocks, rows, HD), f32),
            jax.ShapeDtypeStruct((2 * blocks, 8, rows), f32),
            jax.ShapeDtypeStruct((blocks, rows, HD), jnp.bfloat16),
            jax.ShapeDtypeStruct((blocks, rows, HD), jnp.bfloat16),
            jax.ShapeDtypeStruct((2, blocks, 8, rows), f32),
        )
    else:
        out_shape = (
            jax.ShapeDtypeStruct((units, rows, HD), f32),
            jax.ShapeDtypeStruct((units, 8, rows), f32),
        )
    operands = list(queries) + list(arrays) + list(state or ())
    span = 2048 * len(arrays)
    share = len(distances) / 4.0 * units / 16.0
    return pl.pallas_call(
        functools.partial(attend_kernel, distances, offsets, state is None, last),
        out_shape=out_shape,
        in_specs=[smem_spec(), smem_spec()] + [any_spec()] * len(operands),
        out_specs=tuple(vmem_spec() for _ in out_shape),
        scratch_shapes=[
            pltpu.VMEM((units, rows, HD), jnp.bfloat16),
            pltpu.VMEM((2, span, HD), jnp.bfloat16),
            pltpu.VMEM((2, span, HD), jnp.bfloat16),
            pltpu.VMEM((units, rows, HD), f32),
            pltpu.VMEM((units, 8, rows), f32),
            pltpu.VMEM((rows, HD), f32),
            pltpu.VMEM((rows, HD), f32),
            pltpu.SMEM((12, 17), jnp.int32),
            pltpu.SMEM((12,), jnp.int32),
            pltpu.SemaphoreType.DMA((units,)),
            pltpu.SemaphoreType.DMA((len(arrays), 2, 2)),
            pltpu.SemaphoreType.DMA((2, units)),
        ],
        compiler_params=pltpu.CompilerParams(vmem_limit_bytes=VMEM_LIMIT),
        cost_estimate=pl.CostEstimate(
            flops=int(16e9 * share), bytes_accessed=int((16 << 20) * share), transcendentals=0
        ),
        name="attend",
    )(here, patterns, *operands)


def output_kernel(blocks, splits, own_ref, own_stat, back0_ref, back1_ref, stat0_ref, stat1_ref, weight_ref, *refs):
    outs = refs[:-1]
    joined = refs[-1]
    for at in range(blocks):
        for head in range(2):
            back = (back0_ref, back1_ref)[head]
            stat = (stat0_ref, stat1_ref)[head]
            for part in range(4):
                span = slice(part * BLOCK, (part + 1) * BLOCK)
                high1 = own_stat[head * blocks + at, 0:1, span]
                sum1 = own_stat[head * blocks + at, 1:2, span]
                high2 = stat[at, 0:1, span]
                sum2 = stat[at, 1:2, span]
                top = jnp.maximum(high1, high2)
                scale1 = jnp.exp(high1 - top)
                scale2 = jnp.exp(high2 - top) * sum2
                whole = scale1 * sum1 + scale2
                scale1 = jnp.transpose(jnp.broadcast_to(scale1 / whole, (BLOCK, BLOCK)))
                scale2 = jnp.transpose(jnp.broadcast_to(scale2 / whole, (BLOCK, BLOCK)))
                mixed = (
                    own_ref[head * blocks + at, span, :] * scale1
                    + back[at, span, :].astype(jnp.float32) * scale2
                )
                column = (head * 4 + part) * HD
                joined[at * BLOCK : (at + 1) * BLOCK, column : column + HD] = mixed.astype(
                    jnp.bfloat16
                )
    width = 512
    for at in range(weight_ref.shape[1] // width):
        got = jnp.dot(
            joined[...],
            weight_ref[:, at * width : (at + 1) * width],
            preferred_element_type=jnp.float32,
        )
        for number, (block, begin, end) in enumerate(splits):
            if begin <= at * width < end:
                out = outs[number]
                out[:, at * width - begin : (at + 1) * width - begin] = got[
                    block * BLOCK : (block + 1) * BLOCK, :
                ].astype(out.dtype)


def output(own, own_stat, back0, back1, stat0, stat1, weight, splits):
    blocks = own.shape[0] // 2
    return pl.pallas_call(
        functools.partial(output_kernel, blocks, tuple(s[:3] for s in splits)),
        out_shape=tuple(
            jax.ShapeDtypeStruct((BLOCK, end - begin), dtype) for _, begin, end, dtype in splits
        ),
        in_specs=[vmem_spec()] * 7,
        out_specs=tuple(vmem_spec() for _ in splits),
        scratch_shapes=[pltpu.VMEM((blocks * BLOCK, weight.shape[0]), jnp.bfloat16)],
        compiler_params=pltpu.CompilerParams(vmem_limit_bytes=VMEM_LIMIT),
        cost_estimate=pl.CostEstimate(
            flops=2 * blocks * BLOCK * 1024 * 4096, bytes_accessed=10 << 20, transcendentals=0
        ),
        name="output",
    )(own, own_stat, back0, back1, stat0, stat1, weight)


def per_device(hidden, norm_gain, query_weight, output_weight, cache, pattern):
    corpus = lax.axis_index("corpus")
    tensor = lax.axis_index("tensor")
    my_y, my_x, my_core = corpus // 8, (corpus // 2) % 4, corpus % 2
    here = jnp.stack([my_x, my_y, tensor, my_core]).astype(jnp.int32)

    from_left = shift(query_weight, dx=1)
    from_right = shift(query_weight, dx=-1)
    cache, from_left, from_right = lax.optimization_barrier((cache, from_left, from_right))
    far_low = shift(from_left[:BLOCK], dx=1)
    far_high = shift(from_right[BLOCK:], dx=-1)
    mine = [(query_weight, 0, 0, 0), (from_left, 3, 0, 0), (from_right, 1, 0, 0)]
    mine += [(far_low, 2, 0, 0), (far_high, 2, 0, BLOCK)]
    across = []
    for piece, away, _, _ in mine[:3]:
        across.append((shift(piece[:BLOCK], dy=1), away, 1, 0))
        across.append((shift(piece[BLOCK:], dy=-1), away, 1, BLOCK))
    across.append((shift(far_low, dy=1), 2, 1, 0))
    across.append((shift(far_high, dy=-1), 2, 1, BLOCK))
    mine = mine + across
    pieces, where = [], []
    for piece, away, flip, begin in mine:
        row = (my_y ^ flip) * 4 + (my_x + away) % 4
        pieces.append(piece)
        where.append((row * 2 + my_core) * 256 + begin)
        pieces.append(shift(piece, dk=1))
        where.append((row * 2 + 1 - my_core) * 256 + begin)
    where = jnp.stack(where).astype(jnp.int32)

    cache_left = shift(cache, dx=1)
    cache_right = shift(cache, dx=-1)
    far_keys = shift(cache_left[0], dx=1)
    far_values = shift(cache_right[1], dx=-1)
    near = []
    for held in (cache, cache_left, cache_right):
        near += [held, shift(held, dk=1)]
    far = jnp.stack([far_keys, far_values])
    far = [far, shift(far, dk=1)]

    patterns = jnp.concatenate([pattern, shift(pattern, dy=1), shift(pattern, dy=-1)], axis=0)

    widened = hidden.astype(jnp.float32)
    meansq = jnp.mean(widened * widened, axis=-1, keepdims=True)
    normed = (widened * lax.rsqrt(meansq + 1e-05) * norm_gain.astype(jnp.float32)).astype(
        jnp.bfloat16
    )
    own0, own1 = project(where, normed, pieces)
    other0 = shift(own0, dy=1)
    other1 = shift(own1, dy=-1)
    queries = (own0, own1, other0, other1)

    state = attend(here, patterns, queries, near, (0, 3, 1), (2, 1, 3, 0))
    results = []
    for offsets in ((2,), (1, 3), (0,)):
        own, own_stat, part0, part1, part_stat = attend(
            here, patterns, queries, far, (2,), offsets, state, True
        )
        back0 = shift(part0, dy=-1)
        stat0 = shift(part_stat[0], dy=-1)
        back1 = shift(part1, dy=1)
        stat1 = shift(part_stat[1], dy=1)
        results.append((own, own_stat, back0, back1, stat0, stat1))

    half, full = 2048, 4096
    bf16, f32 = jnp.bfloat16, jnp.float32
    up, down = output(*results[0], output_weight, ((0, 0, half, bf16), (0, half, full, bf16)))
    relay_up = shift(up, dz=1)
    relay_down = shift(down, dz=-1)
    next_low, next_high, back_low, back_high = output(
        *results[1],
        output_weight,
        ((0, 0, half, f32), (0, half, full, bf16), (1, 0, half, bf16), (1, half, full, f32)),
    )
    in_high = shift(next_high, dz=1)
    in_low = shift(back_low, dz=-1)
    next_low = (next_low + relay_up.astype(f32)).astype(bf16)
    back_high = (back_high + relay_down.astype(f32)).astype(bf16)
    in_low2 = shift(next_low, dz=1)
    in_high2 = shift(back_high, dz=-1)
    (rest,) = output(*results[2], output_weight, ((0, 0, full, f32),))
    low = rest[:, :half] + in_low.astype(f32) + in_low2.astype(f32)
    high = rest[:, half:] + in_high.astype(f32) + in_high2.astype(f32)
    return jnp.concatenate([low, high], axis=1).astype(bf16)


def solution(mesh):
    in_specs = (
        P(("dp", "corpus"), None),
        P(),
        P("corpus", "tensor"),
        P("tensor", None),
        P(None, "corpus", "tensor"),
        P(("dp", "corpus"), None),
    )
    out_specs = P(("dp", "corpus", "tensor"), None)
    return jax.shard_map(
        per_device, mesh=mesh, in_specs=in_specs, out_specs=out_specs, check_vma=False
    )
```
